512 devices in a mesh: replica: 64 (over z, y), tensor: 4 (over x), section: 2 (over core).
Axes of the slice: x: 4, y: 4, z: 16, core: 2. Of those that a mesh axis runs over, the one named last changes fastest.
Arguments:
- grads: bfloat16 [64, 2, 1024, 1024], P('replica', 'section', None, 'tensor'), may hold values from -250 to 250
- errors: bfloat16 [64, 2, 1024, 1024], P('replica', 'section', None, 'tensor'), may hold values from -3 to 3
- q_start: float32 [2, 1024, 32], P('section', 'tensor'), may hold values from -6 to 6
- momentum: float32 [2, 1024, 1024], P('section', 'replica', 'tensor'), may hold values from -6 to 6
- vec_grads: float32 [64, 2, 1024], P('replica', 'section', 'tensor'), may hold values from -6 to 6
- vec_momentum: float32 [2, 1024], P('section', 'tensor'), may hold values from -6 to 6
Outputs:
- new_errors: bfloat16 [64, 2, 1024, 1024], P('replica', 'section', None, 'tensor')
- new_momentum: float32 [2, 1024, 1024], P('section', 'replica', 'tensor')
- new_vec_momentum: float32 [2, 1024], P('section', 'tensor')
The draws below stay inside these ranges and needn't reach their ends.
All inputs are finite; a program needn't handle non-finite values.
Results may differ from the reference program's by a relative error of at most 0.0034.
The reference program's roundings to bfloat16 on the way (of `merged`, `q_lo` and `p_lo`) count: a program that leaves them out, or rounds other values in their place, can miss the bound.
Values may be sent and summed in bfloat16 or wider, within the bound.
A program may use at most 64 MiB of HBM per device.

```python
import jax
import jax.numpy as jnp
from jax import lax

D = 1024
RANK = 32
ROUNDS = 2
NB = 2
COLS = 1024
N_REPLICA = 64


def draw_grads(key, part):
    key_one = jax.random.fold_in(key, 11)
    key_two = jax.random.fold_in(key, 12)
    key_three = jax.random.fold_in(key, 13)
    key_four = jax.random.fold_in(key, 14)
    full_shape = (N_REPLICA, NB, D, D)
    row_part = jax.random.normal(key_one, (1, NB, D, 1), jnp.float32)
    col_part = jax.random.normal(key_two, (1, NB, 1, D), jnp.float32)
    common = 0.6 * jax.random.normal(key_three, (1, NB, D, D), jnp.float32) + 0.15 * row_part * col_part
    own_part = jax.random.normal(key_four, full_shape, jnp.float32)
    row_block = jnp.arange(D) // (D // N_REPLICA)
    replica_ids = jnp.arange(N_REPLICA)
    lift_rows = jnp.where(row_block[None, None, :, None] == replica_ids[:, None, None, None], 4.0, 1.0)
    values = common + 0.5 * own_part * lift_rows
    return jnp.clip(values, -250.0, 250.0).astype(jnp.bfloat16)


def steps_of(stream_key, dims, cuts, low, top_value):
    loudness = 1.0
    for position, blocks in cuts:
        heights = jax.random.uniform(jax.random.fold_in(jax.random.fold_in(stream_key, 6), position), (blocks,), jnp.float32, low / len(cuts), top_value / len(cuts))
        loudness = loudness * jnp.repeat(jnp.exp(heights), dims[position] // blocks).reshape((-1,) + (1,) * (len(dims) - 1 - position))
    return loudness


def bell_draw(own_key, shape, width, reach, split=(), held_as=jnp.bfloat16):
    array = jax.random.normal(own_key, shape, jnp.float32) * width
    if len(split) > 0:
        array = steps_of(own_key, shape, split, -0.22, 0.18) * array
    return jnp.clip(array, min=-reach, max=reach).astype(held_as)


def setup_inputs(seed: int = 0) -> dict:
    seeds = jax.random.split(jax.random.key(seed), 7)
    grads = draw_grads(jax.random.fold_in(seeds[6], 71), 0)
    errors = bell_draw(seeds[1], (N_REPLICA, NB, D, COLS), 0.5, 3.0, ((0, 64), (1, 2), (3, 4)))
    q_start = bell_draw(seeds[2], (NB, COLS, RANK), 1.0, 6.0, ((0, 2), (1, 4)), jnp.float32)
    momentum = bell_draw(seeds[3], (NB, D, COLS), 1.0, 6.0, ((0, 2), (1, 64), (2, 4)), jnp.float32)
    vec_grads = bell_draw(seeds[4], (N_REPLICA, NB, COLS), 1.0, 6.0, ((0, 64), (1, 2), (2, 4)), jnp.float32)
    vec_momentum = bell_draw(seeds[5], (NB, COLS), 1.0, 6.0, ((0, 2), (1, 4)), jnp.float32)
    return {"grads": grads, "errors": errors, "q_start": q_start, "momentum": momentum, "vec_grads": vec_grads, "vec_momentum": vec_momentum}


def merge_pair(grad_one, error_one):
    return (grad_one.astype(jnp.float32) + error_one.astype(jnp.float32)).astype(jnp.bfloat16)

def orthonormal(p_sum):
    gram_mat = jnp.einsum('bdr,bds->brs', p_sum, p_sum, precision=lax.Precision.HIGHEST)
    factor = jnp.linalg.cholesky(gram_mat)

    def solve_one(lower, matrix):
        return jax.scipy.linalg.solve_triangular(lower, matrix.T, lower=True).T
    return jax.vmap(solve_one)(factor, p_sum)

def reference(grads, errors, q_start, momentum, vec_grads, vec_momentum):
    q_lo = q_start.astype(jnp.bfloat16)
    p_lo = None
    for round_no in range(ROUNDS):

        def add_left(total, pieces):
            merged = merge_pair(pieces[0], pieces[1])
            return (total + jnp.einsum('bdc,bcr->bdr', merged.astype(jnp.float32), q_lo.astype(jnp.float32)), None)
        p_zero = jnp.zeros((NB, D, RANK), jnp.float32)
        p_sum = lax.scan(add_left, p_zero, (grads, errors))[0] / N_REPLICA
        p_lo = orthonormal(p_sum).astype(jnp.bfloat16)

        def add_right(total, pieces):
            merged = merge_pair(pieces[0], pieces[1])
            return (total + jnp.einsum('bdc,bdr->bcr', merged.astype(jnp.float32), p_lo.astype(jnp.float32)), None)
        q_zero = jnp.zeros((NB, COLS, RANK), jnp.float32)
        q_sum = lax.scan(add_right, q_zero, (grads, errors))[0] / N_REPLICA
        q_lo = q_sum.astype(jnp.bfloat16)
    approx = jnp.einsum('bdr,bcr->bdc', p_lo.astype(jnp.float32), q_lo.astype(jnp.float32))

    def error_one(pieces):
        merged = merge_pair(pieces[0], pieces[1])
        return (merged.astype(jnp.float32) - approx).astype(jnp.bfloat16)
    new_errors = lax.map(error_one, (grads, errors))
    new_momentum = 0.9 * momentum + approx
    new_vec_momentum = 0.9 * vec_momentum + jnp.sum(vec_grads, axis=0) / N_REPLICA
    return (new_errors, new_momentum, new_vec_momentum)
```

```python
import functools

import jax
import jax.numpy as jnp
from jax import lax
from jax.experimental import pallas as pl
from jax.experimental.pallas import tpu as pltpu
from jax.sharding import PartitionSpec as P

NX, NY, NZ = 4, 4, 16
RANK = 32
MESH = pl.DeviceIdType.MESH
F32, BF16 = jnp.float32, jnp.bfloat16
HIGHEST = lax.Precision.HIGHEST


def ring(d, n):
    return min(d, n - d)


XY = sorted(
    ((a, b) for a in range(NX) for b in range(NY) if (a, b) != (0, 0)),
    key=lambda o: -(ring(o[0], NX) + ring(o[1], NY)),
)
ZS = sorted(range(1, NZ), key=lambda c: -ring(c, NZ))
YS = (2, 1, 3)


def nt(a, b, precision=None):
    return lax.dot_general(a, b, (((1,), (1,)), ((), ())), precision=precision, preferred_element_type=F32)


def tn(a, b):
    return lax.dot_general(a, b, (((0,), (0,)), ((), ())), preferred_element_type=F32)


def total(ref, n):
    parts = [ref[i].astype(F32) for i in range(n)]
    while len(parts) > 1:
        parts = [parts[i] + parts[i + 1] for i in range(0, len(parts), 2)]
    return parts[0]


def orthonormal(p):
    gram = nt(p, p, HIGHEST)
    row = lax.broadcasted_iota(jnp.int32, (RANK, RANK), 0)
    col = lax.broadcasted_iota(jnp.int32, (RANK, RANK), 1)
    diag = row == col
    a = jnp.concatenate([gram, jnp.where(diag, 1.0, 0.0).astype(F32)], axis=1)
    rows = lax.broadcasted_iota(jnp.int32, (RANK, 1), 0)
    for k in range(RANK - 1):
        r = a[k : k + 1, :] / a[k : k + 1, k : k + 1]
        c = jnp.where(rows > k, a[:, k : k + 1], 0.0)
        a = a - c * r
    d = jnp.sum(jnp.where(diag, a[:, :RANK], 0.0), axis=1, keepdims=True)
    inverse = a[:, RANK:] / jnp.sqrt(d)
    return lax.dot_general(inverse, p, (((1,), (0,)), ((), ())), precision=HIGHEST, preferred_element_type=F32)


def kernel(
    g_hbm, e_hbm, q_ref, mom_ref, vg_ref, vm_ref,
    ne_hbm, nm_ref, nv_ref,
    gbuf, ebuf, merged, ybuf, ysum, zbuf, msum, mfull, mhi, mlo,
    p1part, p1rs, p1mid, p1z, p1own, pt, p2part, p2buf, plo, qpart, qbuf, qlo,
    vybuf, vysum, vzbuf, approx, outbuf,
    load_sem, out_sem, y_s, y_r, vy_s, vy_r, z_s, z_r, vz_s, vz_r, a_s, a_r,
    p1_s, p1_r, p1z_s, p1z_r, p1a_s, p1a_r, p2_s, p2_r, q_s, q_r,
):
    rep = lax.axis_index("replica")
    x = lax.axis_index("tensor")
    sec = lax.axis_index("section")
    z, y = rep // NY, rep % NY
    replicas = NY * NZ
    rows = merged.shape[0]
    yrows = rows // NY
    zrows = yrows // NZ

    def at_xy(a, b):
        xx, yy = lax.rem(x + a, NX), lax.rem(y + b, NY)
        return xx, yy, (z * NY + yy, xx, sec)

    def at_z(c):
        zz = lax.rem(z + c, NZ)
        return zz, (zz * NY + y, x, sec)

    def send(src, dst, ssem, rsem, dev):
        c = pltpu.make_async_remote_copy(
            src_ref=src, dst_ref=dst, send_sem=ssem, recv_sem=rsem, device_id=dev, device_id_type=MESH
        )
        c.start()
        return c

    loads = []
    for i in range(NY):
        part = pl.ds(i * yrows, yrows)
        loads.append(pltpu.make_async_copy(g_hbm.at[0, 0, part], gbuf.at[part], load_sem.at[0, i]))
        loads.append(pltpu.make_async_copy(e_hbm.at[0, 0, part], ebuf.at[part], load_sem.at[1, i]))
    for c in loads:
        c.start()

    barrier = pltpu.get_barrier_semaphore()
    for c in ZS:
        pl.semaphore_signal(barrier, inc=1, device_id=at_z(c)[1], device_id_type=MESH)
    for a, b in XY:
        pl.semaphore_signal(barrier, inc=1, device_id=at_xy(a, b)[2], device_id_type=MESH)

    qlo[0] = q_ref[0].astype(BF16)
    for i in range(NY):
        loads[2 * i].wait()
        loads[2 * i + 1].wait()
        part = pl.ds(i * yrows, yrows)
        m = (gbuf[part, :].astype(F32) + ebuf[part, :].astype(F32)).astype(BF16)
        merged[part, :] = m
        p1part[:, part] = nt(qlo[0], m)

    pl.semaphore_wait(barrier, len(ZS) + len(XY))

    def chunk(xx, yy):
        k = xx * NY + yy
        return (
            pl.ds(pl.multiple_of(lax.rem(k, 2) * 16, 16), 16),
            pl.ds(pl.multiple_of((k // 2) * 128, 128), 128),
        )

    p1 = []
    me_xy = x * NY + y
    for j, (a, b) in enumerate(XY):
        xx, yy, dev = at_xy(a, b)
        s, l = chunk(xx, yy)
        p1.append(send(p1part.at[s, l], p1rs.at[me_xy], p1_s.at[j], p1_r.at[j], dev))
    ys, vys = [], []
    for j, b in enumerate(YS):
        xx, yy, dev = at_xy(0, b)
        ys.append(
            send(merged.at[pl.ds(pl.multiple_of(yy * yrows, yrows), yrows)], ybuf.at[y], y_s.at[j], y_r.at[j], dev)
        )
        vys.append(send(vg_ref.at[0], vybuf.at[y], vy_s.at[j], vy_r.at[j], dev))
    own_s, own_l = chunk(x, y)
    p1rs[me_xy] = p1part[own_s, own_l]
    ybuf[y] = merged[pl.ds(pl.multiple_of(y * yrows, yrows), yrows), :]
    vybuf[y] = vg_ref[0]

    for c in p1:
        c.wait()
    mid = total(p1rs, NX * NY)
    p1mid[...] = mid
    p1z[z] = mid
    p1zs = []
    for j, c in enumerate(ZS):
        zz, dev = at_z(c)
        p1zs.append(send(p1mid, p1z.at[z], p1z_s.at[j], p1z_r.at[j], dev))

    for c in ys + vys:
        c.wait()
    ysum[...] = total(ybuf, NY)
    v = total(vybuf, NY)
    vysum[...] = v
    vzbuf[z] = v
    zs, vzs = [], []
    for j, c in enumerate(ZS):
        zz, dev = at_z(c)
        zs.append(
            send(ysum.at[pl.ds(pl.multiple_of(zz * zrows, zrows), zrows)], zbuf.at[z], z_s.at[j], z_r.at[j], dev)
        )
        vzs.append(send(vysum, vzbuf.at[z], vz_s.at[j], vz_r.at[j], dev))
    my_z = pl.ds(pl.multiple_of(z * zrows, zrows), zrows)
    zbuf[z] = ysum[my_z, :]

    for c in p1zs:
        c.wait()
    own = total(p1z, NZ)
    p1own[...] = own
    pt[own_s, own_l] = own
    p1as = []
    for j, (a, b) in enumerate(XY):
        xx, yy, dev = at_xy(a, b)
        p1as.append(send(p1own, pt.at[own_s, own_l], p1a_s.at[j], p1a_r.at[j], dev))

    for c in zs:
        c.wait()
    mz = total(zbuf, NZ)
    msum[...] = mz
    mfull[my_z, :] = mz
    ags = []
    for j, c in enumerate(ZS):
        zz, dev = at_z(c)
        ags.append(send(msum, mfull.at[my_z], a_s.at[j], a_r.at[j], dev))

    for c in vzs:
        c.wait()
    nv_ref[...] = 0.9 * vm_ref[...] + total(vzbuf, NZ) / replicas

    for c in p1as:
        c.wait()
    plo[...] = orthonormal(pt[...] / replicas).astype(BF16)

    for c in ags:
        c.wait()
    m = mfull[...]
    hi = m.astype(BF16)
    mhi[...] = hi
    mlo[...] = (m - hi.astype(F32)).astype(BF16)

    def right(n):
        mine = plo[:, pl.ds(pl.multiple_of(y * yrows, yrows), yrows)]
        part = jnp.dot(mine, mhi[...], preferred_element_type=F32) + jnp.dot(
            mine, mlo[...], preferred_element_type=F32
        )
        qpart[n] = part
        qbuf[n, y] = part
        cs = []
        for j, b in enumerate(YS):
            cs.append(send(qpart.at[n], qbuf.at[n, y], q_s.at[n, j], q_r.at[n, j], at_xy(0, b)[2]))
        for c in cs:
            c.wait()
        qlo[n + 1] = (total(qbuf.at[n], NY) / replicas).astype(BF16)

    right(0)

    part = nt(qlo[1], mhi[...]) + nt(qlo[1], mlo[...])
    p2part[...] = part
    p2buf[y, x] = part
    cs = []
    for j, (a, b) in enumerate(XY):
        cs.append(send(p2part, p2buf.at[y, x], p2_s.at[j], p2_r.at[j], at_xy(a, b)[2]))
    for c in cs:
        c.wait()
    for i in range(NY):
        pt[:, pl.ds(i * yrows, yrows)] = total(p2buf.at[i], NX)
    plo[...] = orthonormal(pt[...] / replicas).astype(BF16)

    right(1)

    outs = []
    for i in range(NY):
        part = pl.ds(i * yrows, yrows)
        ap = tn(plo[:, part], qlo[2])
        approx[part, :] = ap
        outbuf[part, :] = (merged[part, :].astype(F32) - ap).astype(BF16)
        c = pltpu.make_async_copy(outbuf.at[part], ne_hbm.at[0, 0, part], out_sem.at[i])
        c.start()
        outs.append(c)
    own_rows = nm_ref.shape[1]
    nm_ref[0] = 0.9 * mom_ref[0] + approx[pl.ds(pl.multiple_of(rep * own_rows, own_rows), own_rows), :]
    for c in outs:
        c.wait()


def body(grads, errors, q_start, momentum, vec_grads, vec_momentum):
    rows, cols = grads.shape[2:]
    yrows, zrows = rows // NY, rows // NY // NZ
    nxy, nz = len(XY), len(ZS)
    vmem, dma = pltpu.VMEM, pltpu.SemaphoreType.DMA
    in_vmem = pl.BlockSpec(memory_space=pltpu.VMEM)
    in_any = pl.BlockSpec(memory_space=pl.ANY)
    sds = jax.ShapeDtypeStruct
    return pl.pallas_call(
        kernel,
        out_shape=(
            sds(grads.shape, BF16),
            sds(momentum.shape, F32),
            sds(vec_momentum.shape, F32),
        ),
        in_specs=[in_any, in_any] + [in_vmem] * 4,
        out_specs=(in_any, in_vmem, in_vmem),
        scratch_shapes=[
            vmem((rows, cols), BF16),
            vmem((rows, cols), BF16),
            vmem((rows, cols), BF16),
            vmem((NY, yrows, cols), BF16),
            vmem((yrows, cols), F32),
            vmem((NZ, zrows, cols), F32),
            vmem((zrows, cols), F32),
            vmem((yrows, cols), F32),
            vmem((yrows, cols), BF16),
            vmem((yrows, cols), BF16),
            vmem((RANK, rows), F32),
            vmem((NX * NY, 16, 128), F32),
            vmem((16, 128), F32),
            vmem((NZ, 16, 128), F32),
            vmem((16, 128), F32),
            vmem((RANK, rows), F32),
            vmem((RANK, yrows), F32),
            vmem((NY, NX, RANK, yrows), F32),
            vmem((RANK, rows), BF16),
            vmem((2, RANK, cols), F32),
            vmem((2, NY, RANK, cols), F32),
            vmem((3, RANK, cols), BF16),
            vmem((NY, 1, cols), F32),
            vmem((1, cols), F32),
            vmem((NZ, 1, cols), F32),
            vmem((rows, cols), F32),
            vmem((rows, cols), BF16),
            dma((2, NY)), dma((NY,)),
            dma((3,)), dma((3,)), dma((3,)), dma((3,)),
            dma((nz,)), dma((nz,)), dma((nz,)), dma((nz,)), dma((nz,)), dma((nz,)),
            dma((nxy,)), dma((nxy,)), dma((nz,)), dma((nz,)), dma((nxy,)), dma((nxy,)),
            dma((nxy,)), dma((nxy,)), dma((2, 3)), dma((2, 3)),
        ],
        compiler_params=pltpu.CompilerParams(collective_id=0, has_side_effects=True),
        name="powersgd",
    )(grads, errors, jnp.swapaxes(q_start, 1, 2), momentum, vec_grads, vec_momentum)


def solution(mesh):
    placed = (
        P("replica", "section", None, "tensor"),
        P("replica", "section", None, "tensor"),
        P("section", "tensor", None),
        P("section", "replica", "tensor"),
        P("replica", "section", "tensor"),
        P("section", "tensor"),
    )
    return jax.shard_map(
        body,
        mesh=mesh,
        in_specs=placed,
        out_specs=(
            P("replica", "section", None, "tensor"),
            P("section", "replica", "tensor"),
            P("section", "tensor"),
        ),
        check_vma=False,
    )
```

```python
import functools

import jax
import jax.numpy as jnp
from jax import lax
from jax.experimental import pallas as pl
from jax.experimental.pallas import tpu as pltpu
from jax.sharding import PartitionSpec as P

NX, NY, NZ = 4, 4, 16
RANK = 32
MESH = pl.DeviceIdType.MESH
F32, BF16 = jnp.float32, jnp.bfloat16
HIGHEST = lax.Precision.HIGHEST


def ring(d, n):
    return min(d, n - d)


XY = sorted(
    ((a, b) for a in range(NX) for b in range(NY) if (a, b) != (0, 0)),
    key=lambda o: -(ring(o[0], NX) + ring(o[1], NY)),
)
ZS = sorted(range(1, NZ), key=lambda c: -ring(c, NZ))
YS = (2, 1, 3)


def nt(a, b, precision=None):
    return lax.dot_general(a, b, (((1,), (1,)), ((), ())), precision=precision, preferred_element_type=F32)


def tn(a, b):
    return lax.dot_general(a, b, (((0,), (0,)), ((), ())), preferred_element_type=F32)


def total(ref, n):
    parts = [ref[i].astype(F32) for i in range(n)]
    while len(parts) > 1:
        parts = [parts[i] + parts[i + 1] for i in range(0, len(parts), 2)]
    return parts[0]


def orthonormal(gram, p):
    row = lax.broadcasted_iota(jnp.int32, (RANK, RANK), 0)
    col = lax.broadcasted_iota(jnp.int32, (RANK, RANK), 1)
    diag = row == col
    a = jnp.concatenate([gram, jnp.where(diag, 1.0, 0.0).astype(F32)], axis=1)
    rows = lax.broadcasted_iota(jnp.int32, (RANK, 1), 0)
    for k in range(RANK - 1):
        r = a[k : k + 1, :] / a[k : k + 1, k : k + 1]
        c = jnp.where(rows > k, a[:, k : k + 1], 0.0)
        a = a - c * r
    d = jnp.sum(jnp.where(diag, a[:, :RANK], 0.0), axis=1, keepdims=True)
    inverse = a[:, RANK:] / jnp.sqrt(d)
    return lax.dot_general(inverse, p, (((1,), (0,)), ((), ())), precision=HIGHEST, preferred_element_type=F32)


def kernel(
    g_hbm, e_hbm, q_hbm, vg_hbm, vm_hbm,
    merged, plo, qlo_out, nv_ref,
    gbuf, ebuf, qstart, vgrad, vmom, ybuf, ysum, zbuf, msum, mfull, mhi, mlo,
    p1part, p1rs, p1mid, p1z, p1own, pt, p2part, p2buf, gpart, grams, pmine, qpart, qbuf, qlo,
    vybuf, vysum, vzbuf,
    load_sem, small_sem, y_s, y_r, vy_s, vy_r, z_s, z_r, vz_s, vz_r, a_s, a_r,
    p1_s, p1_r, p1z_s, p1z_r, p1a_s, p1a_r, p2_s, p2_r, g_s, g_r, pl_s, pl_r, q_s, q_r,
):
    rep = lax.axis_index("replica")
    x = lax.axis_index("tensor")
    sec = lax.axis_index("section")
    z, y = rep // NY, rep % NY
    replicas = NY * NZ
    rows = merged.shape[0]
    yrows = rows // NY
    zrows = yrows // NZ

    def at_xy(a, b):
        xx, yy = lax.rem(x + a, NX), lax.rem(y + b, NY)
        return xx, yy, (z * NY + yy, xx, sec)

    def at_z(c):
        zz = lax.rem(z + c, NZ)
        return zz, (zz * NY + y, x, sec)

    def send(src, dst, ssem, rsem, dev):
        c = pltpu.make_async_remote_copy(
            src_ref=src, dst_ref=dst, send_sem=ssem, recv_sem=rsem, device_id=dev, device_id_type=MESH
        )
        c.start()
        return c

    load_q = pltpu.make_async_copy(q_hbm.at[0], qstart, small_sem.at[0])
    load_v = pltpu.make_async_copy(vg_hbm.at[0], vgrad, small_sem.at[1])
    load_vm = pltpu.make_async_copy(vm_hbm, vmom, small_sem.at[2])
    loads = []
    for i in range(NY):
        part = pl.ds(i * yrows, yrows)
        loads.append(pltpu.make_async_copy(g_hbm.at[0, 0, part], gbuf.at[part], load_sem.at[0, i]))
        loads.append(pltpu.make_async_copy(e_hbm.at[0, 0, part], ebuf.at[part], load_sem.at[1, i]))
    barrier = pltpu.get_barrier_semaphore()
    for c in ZS:
        pl.semaphore_signal(barrier, inc=1, device_id=at_z(c)[1], device_id_type=MESH)
    for a, b in XY:
        pl.semaphore_signal(barrier, inc=1, device_id=at_xy(a, b)[2], device_id_type=MESH)
    for c in [load_q, load_v, load_vm] + loads:
        c.start()

    load_q.wait()
    load_v.wait()
    load_vm.wait()
    qlo[0] = qstart[...].astype(BF16)
    for i in range(NY):
        loads[2 * i].wait()
        loads[2 * i + 1].wait()
        part = pl.ds(i * yrows, yrows)
        m = (gbuf[part, :].astype(F32) + ebuf[part, :].astype(F32)).astype(BF16)
        merged[part, :] = m
        p1part[:, part] = nt(qlo[0], m)

    my_y = pl.ds(pl.multiple_of(y * yrows, yrows), yrows)
    my_z = pl.ds(pl.multiple_of(z * zrows, zrows), zrows)

    def chunk(xx, yy):
        k = xx * NY + yy
        return (
            pl.ds(pl.multiple_of(lax.rem(k, 2) * 16, 16), 16),
            pl.ds(pl.multiple_of((k // 2) * 128, 128), 128),
        )

    me_xy = x * NY + y
    own_s, own_l = chunk(x, y)
    p1rs[me_xy] = p1part[own_s, own_l]
    ybuf[y] = merged[my_y, :]
    vybuf[y] = vgrad[...]

    pl.semaphore_wait(barrier, len(ZS) + len(XY))

    ys, vys, p1 = [], [], []
    for j, b in enumerate(YS):
        xx, yy, dev = at_xy(0, b)
        ys.append(
            send(merged.at[pl.ds(pl.multiple_of(yy * yrows, yrows), yrows)], ybuf.at[y], y_s.at[j], y_r.at[j], dev)
        )
        vys.append(send(vgrad, vybuf.at[y], vy_s.at[j], vy_r.at[j], dev))
    for j, (a, b) in enumerate(XY):
        xx, yy, dev = at_xy(a, b)
        s, l = chunk(xx, yy)
        p1.append(send(p1part.at[s, l], p1rs.at[me_xy], p1_s.at[j], p1_r.at[j], dev))

    for c in ys + vys:
        c.wait()
    ysum[...] = total(ybuf, NY).astype(BF16)
    v = total(vybuf, NY)
    vysum[...] = v
    vzbuf[z] = v
    zs, vzs = [], []
    for j, c in enumerate(ZS):
        zz, dev = at_z(c)
        zs.append(
            send(ysum.at[pl.ds(pl.multiple_of(zz * zrows, zrows), zrows)], zbuf.at[z], z_s.at[j], z_r.at[j], dev)
        )
    zbuf[z] = ysum[my_z, :]

    for c in p1:
        c.wait()
    mid = total(p1rs, NX * NY)
    p1mid[...] = mid
    p1z[z] = mid
    p1zs = []
    for j, c in enumerate(ZS):
        zz, dev = at_z(c)
        p1zs.append(send(p1mid, p1z.at[z], p1z_s.at[j], p1z_r.at[j], dev))

    for c in zs:
        c.wait()
    mz = total(zbuf, NZ)
    msum[...] = mz
    mfull[my_z, :] = mz
    ags = []
    for j, c in enumerate(ZS):
        zz, dev = at_z(c)
        ags.append(send(msum, mfull.at[my_z], a_s.at[j], a_r.at[j], dev))

    for c in p1zs:
        c.wait()
    own = total(p1z, NZ)
    p1own[...] = own
    pt[own_s, own_l] = own
    p1as = []
    for j, (a, b) in enumerate(XY):
        xx, yy, dev = at_xy(a, b)
        p1as.append(send(p1own, pt.at[own_s, own_l], p1a_s.at[j], p1a_r.at[j], dev))
    for j, c in enumerate(ZS):
        zz, dev = at_z(c)
        vzs.append(send(vysum, vzbuf.at[z], vz_s.at[j], vz_r.at[j], dev))

    for c in p1as:
        c.wait()
    p = pt[...] / replicas
    pt[...] = p
    mine = pt[:, my_y]
    pmine[0] = orthonormal(nt(p, p, HIGHEST), mine).astype(BF16)

    for c in ags:
        c.wait()
    m = mfull[...]
    hi = m.astype(BF16)
    mhi[...] = hi
    mlo[...] = (m - hi.astype(F32)).astype(BF16)

    def right(n):
        part = jnp.dot(pmine[n], mhi[...], preferred_element_type=F32) + jnp.dot(
            pmine[n], mlo[...], preferred_element_type=F32
        )
        qpart[n] = part
        qbuf[n, y] = part
        cs = []
        for j, b in enumerate(YS):
            cs.append(send(qpart.at[n], qbuf.at[n, y], q_s.at[n, j], q_r.at[n, j], at_xy(0, b)[2]))
        return cs

    def right_sum(n, cs):
        for c in cs:
            c.wait()
        return (total(qbuf.at[n], NY) / replicas).astype(BF16)

    qlo[1] = right_sum(0, right(0))

    part = nt(qlo[1], mhi[...]) + nt(qlo[1], mlo[...])
    p2part[...] = part
    p2buf[x] = part
    cs = []
    for j, a in enumerate(YS):
        cs.append(send(p2part, p2buf.at[x], p2_s.at[j], p2_r.at[j], at_xy(a, 0)[2]))
    for c in cs:
        c.wait()
    mine = total(p2buf, NX) / replicas
    part = nt(mine, mine, HIGHEST)
    gpart[...] = part
    grams[y] = part
    cs = []
    for j, b in enumerate(YS):
        cs.append(send(gpart, grams.at[y], g_s.at[j], g_r.at[j], at_xy(0, b)[2]))
    for c in cs:
        c.wait()
    last = orthonormal(total(grams, NY), mine).astype(BF16)
    pmine[1] = last
    plo[:, my_y] = last

    cs = right(1)
    pls = []
    for j, b in enumerate(YS):
        pls.append(send(pmine.at[1], plo.at[:, my_y], pl_s.at[j], pl_r.at[j], at_xy(0, b)[2]))
    for c in vzs:
        c.wait()
    nv_ref[...] = 0.9 * vmom[...] + total(vzbuf, NZ) / replicas
    qlo_out[...] = right_sum(1, cs)
    for c in pls:
        c.wait()


def finish(merged, plo, qlo, nv, mom_ref, ne_hbm, nm_hbm, nv_hbm, approx, outbuf, nm, out_sem, nm_sem, nv_sem):
    rep = lax.axis_index("replica")
    rows = merged.shape[0]
    step = rows // NY
    outs = [pltpu.make_async_copy(nv, nv_hbm, nv_sem)]
    outs[0].start()
    for i in range(NY):
        part = pl.ds(i * step, step)
        ap = tn(plo[:, part], qlo[...])
        approx[part, :] = ap
        outbuf[part, :] = (merged[part, :].astype(F32) - ap).astype(BF16)
        c = pltpu.make_async_copy(outbuf.at[part], ne_hbm.at[0, 0, part], out_sem.at[i])
        c.start()
        outs.append(c)
    own = nm.shape[0]
    nm[...] = 0.9 * mom_ref[0] + approx[pl.ds(pl.multiple_of(rep * own, own), own), :]
    c = pltpu.make_async_copy(nm, nm_hbm.at[0], nm_sem)
    c.start()
    outs.append(c)
    for c in outs:
        c.wait()


def body(grads, errors, q_start, momentum, vec_grads, vec_momentum):
    rows, cols = grads.shape[2:]
    yrows, zrows = rows // NY, rows // NY // NZ
    nxy, nz = len(XY), len(ZS)
    vmem, dma = pltpu.VMEM, pltpu.SemaphoreType.DMA
    in_vmem = pl.BlockSpec(memory_space=pltpu.VMEM)
    in_hbm = pl.BlockSpec(memory_space=pltpu.HBM)
    sds = jax.ShapeDtypeStruct
    merged, plo, qlo, new_vec = pl.pallas_call(
        kernel,
        out_shape=(
            sds((rows, cols), BF16),
            sds((RANK, rows), BF16),
            sds((RANK, cols), BF16),
            sds(vec_momentum.shape, F32),
        ),
        in_specs=[in_hbm] * 5,
        out_specs=(in_vmem,) * 4,
        scratch_shapes=[
            vmem((rows, cols), BF16),
            vmem((rows, cols), BF16),
            vmem((RANK, cols), F32),
            vmem((1, cols), F32),
            vmem((1, cols), F32),
            vmem((NY, yrows, cols), BF16),
            vmem((yrows, cols), BF16),
            vmem((NZ, zrows, cols), BF16),
            vmem((zrows, cols), F32),
            vmem((yrows, cols), F32),
            vmem((yrows, cols), BF16),
            vmem((yrows, cols), BF16),
            vmem((RANK, rows), F32),
            vmem((NX * NY, 16, 128), F32),
            vmem((16, 128), F32),
            vmem((NZ, 16, 128), F32),
            vmem((16, 128), F32),
            vmem((RANK, rows), F32),
            vmem((RANK, yrows), F32),
            vmem((NX, RANK, yrows), F32),
            vmem((RANK, RANK), F32),
            vmem((NY, RANK, RANK), F32),
            vmem((2, RANK, yrows), BF16),
            vmem((2, RANK, cols), F32),
            vmem((2, NY, RANK, cols), F32),
            vmem((2, RANK, cols), BF16),
            vmem((NY, 1, cols), F32),
            vmem((1, cols), F32),
            vmem((NZ, 1, cols), F32),
            dma((2, NY)), dma((3,)),
            dma((3,)), dma((3,)), dma((3,)), dma((3,)),
            dma((nz,)), dma((nz,)), dma((nz,)), dma((nz,)), dma((nz,)), dma((nz,)),
            dma((nxy,)), dma((nxy,)), dma((nz,)), dma((nz,)), dma((nxy,)), dma((nxy,)),
            dma((3,)), dma((3,)), dma((3,)), dma((3,)), dma((3,)), dma((3,)), dma((2, 3)), dma((2, 3)),
        ],
        compiler_params=pltpu.CompilerParams(collective_id=0, has_side_effects=True, vmem_limit_bytes=16 * 1024 * 1024),
        name="powersgd",
    )(*(pltpu.with_memory_space_constraint(a, pltpu.HBM) for a in (grads, errors, jnp.swapaxes(q_start, 1, 2), vec_grads, vec_momentum)))
    return pl.pallas_call(
        finish,
        out_shape=(
            sds(grads.shape, BF16),
            sds(momentum.shape, F32),
            sds(vec_momentum.shape, F32),
        ),
        in_specs=[in_vmem] * 5,
        out_specs=(in_hbm,) * 3,
        scratch_shapes=[
            vmem((rows, cols), F32),
            vmem((rows, cols), BF16),
            vmem(momentum.shape[1:], F32),
            dma((NY,)), dma, dma,
        ],
        compiler_params=pltpu.CompilerParams(vmem_limit_bytes=8 * 1024 * 1024),
        name="finish",
    )(merged, plo, qlo, new_vec, momentum)


def solution(mesh):
    placed = (
        P("replica", "section", None, "tensor"),
        P("replica", "section", None, "tensor"),
        P("section", "tensor", None),
        P("section", "replica", "tensor"),
        P("replica", "section", "tensor"),
        P("section", "tensor"),
    )
    return jax.shard_map(
        body,
        mesh=mesh,
        in_specs=placed,
        out_specs=(
            P("replica", "section", None, "tensor"),
            P("section", "replica", "tensor"),
            P("section", "tensor"),
        ),
        check_vma=False,
    )
```
